32 devices in a mesh: dp: 8 (over z, y), tensor: 4 (over x, core).
Axes of the slice: x: 2, y: 2, z: 4, core: 2. Of those that a mesh axis runs over, the one named last changes fastest.
Arguments:
- inputs: bfloat16 [8192, 2048], P('dp'), may hold values from -6 to 6
- teacher: bfloat16 [8192, 2048], P('dp', 'tensor'), may hold values from -6 to 6
- lengths: int32 [8], P('dp'), may hold values from 213 to 1024, as said below
- gain_one: float32 [2048], replicated, may hold values from 0.5 to 1.5
- w_query_down: bfloat16 [2048, 1024], P(None, 'tensor'), may hold values from -0.125 to 0.125
- gain_query: float32 [1024], replicated, may hold values from 0.5 to 1.5
- w_query_up: bfloat16 [1024, 4096], P(None, 'tensor'), may hold values from -0.375 to 0.375
- w_keyvalue: bfloat16 [2048, 512], replicated, may hold values from -0.125 to 0.125
- w_output: bfloat16 [4096, 2048], P('tensor'), may hold values from -0.75 to 0.75
- gain_two: float32 [2048], replicated, may hold values from 0.5 to 1.5
- w_gate: bfloat16 [2048, 5632], P(None, 'tensor'), may hold values from -0.125 to 0.125
- w_up: bfloat16 [2048, 5632], P(None, 'tensor'), may hold values from -0.125 to 0.125
- w_down: bfloat16 [5632, 2048], P('tensor'), may hold values from -0.078125 to 0.078125
Outputs:
- output: bfloat16 [8192, 2048], P('dp', 'tensor')
- layer_loss: float32 [], replicated
- input_grad: bfloat16 [8192, 2048], P('dp', 'tensor')
- grad_gain_one: float32 [2048], P('tensor')
- grad_w_query_down: float32 [2048, 1024], P(None, 'tensor')
- grad_gain_query: float32 [1024], P('tensor')
- grad_w_query_up: float32 [1024, 4096], P(None, 'tensor')
- grad_w_keyvalue: float32 [2048, 512], P(None, 'tensor')
- grad_w_output: float32 [4096, 2048], P('tensor')
- grad_gain_two: float32 [2048], P('tensor')
- grad_w_gate: float32 [2048, 5632], P(None, 'tensor')
- grad_w_up: float32 [2048, 5632], P(None, 'tensor')
- grad_w_down: float32 [5632, 2048], P('tensor')
The draws below stay inside these ranges and needn't reach their ends.
Inputs may be any that keep to these rules, and one draw needn't show every extreme that they name: `lengths`: valid tokens fill the first slots of their sequence; the last sequence has all 1024.
All inputs are finite; a program needn't handle non-finite values.
Results may differ from the reference program's by a relative error of at most 0.03.
Values may be sent and summed in bfloat16 or wider, within the bound.
A program may use at most 256 MiB of HBM per device.

```python
import math
import jax
import jax.numpy as jnp
from jax import lax

D = 2048
RANK = 1024
HEADS = 16
HD = 256
FF = 5632
LEN = 1024
SEQS = 8
TOKENS = 8192
N_TENSOR = 4


def draw_lengths(key, part):
    sequence_index = jnp.arange(SEQS, dtype=jnp.int32)
    middle_length = LEN // 3 + (LEN - LEN // 3) * sequence_index // max(SEQS - 1, 1)
    low_end = jnp.maximum(middle_length - LEN // 8, 1)
    drawn_lengths = jax.random.randint(key, (SEQS,), low_end, middle_length + 1)
    drawn_lengths = jnp.where(sequence_index == 0, low_end, drawn_lengths)
    return jnp.where(sequence_index == SEQS - 1, LEN, drawn_lengths).astype(jnp.int32)


def shard_levels(stream_key, dims, shards, smallest, largest):
    factor_of, own = 1.0, jax.random.fold_in(stream_key, 6)
    for position, shards_of in shards:
        draws = jnp.exp(jax.random.uniform(jax.random.fold_in(own, position), (shards_of,), jnp.float32, smallest / len(shards), largest / len(shards)))
        factor_of = factor_of * jnp.repeat(draws, dims[position] // shards_of).reshape([-1 if axis == position else 1 for axis in range(len(dims))])
    return factor_of


def noise(rng, shape, scale, limit, shards=(), kind=jnp.bfloat16):
    result = scale * jax.random.normal(rng, shape, jnp.float32)
    if shards:
        result = result * shard_levels(rng, shape, shards, -0.22, 0.18)
    return jnp.clip(result, -limit, limit).astype(kind)


def setup_inputs(seed: int = 0) -> dict:
    key_list = jax.random.split(jax.random.key(seed), 14)
    inputs = noise(key_list[0], (TOKENS, D), 1.0, 6.0, ((0, 8),))
    teacher = noise(key_list[1], (TOKENS, D), 1.0, 6.0, ((0, 8), (1, 4)))
    lengths = draw_lengths(jax.random.fold_in(key_list[13], 71), 0)
    gain_one = jnp.clip(1.0 + 0.1 * jax.random.normal(key_list[3], (D,), jnp.float32), 0.5, 1.5)
    w_query_down = noise(key_list[4], (D, RANK), D ** -0.5, 0.125, ((1, 4),))
    gain_query = jnp.clip(1.0 + 0.1 * jax.random.normal(key_list[5], (RANK,), jnp.float32), 0.5, 1.5)
    w_query_up = noise(key_list[6], (RANK, HEADS * HD), (RANK // 4) ** -0.5, 0.375, ((1, 4),))
    w_keyvalue = noise(key_list[7], (D, 2 * HD), D ** -0.5, 0.125)
    w_output = noise(key_list[8], (HEADS * HD, D), (HEADS * HD // 64) ** -0.5, 0.75, ((0, 4),))
    gain_two = jnp.clip(1.0 + 0.1 * jax.random.normal(key_list[9], (D,), jnp.float32), 0.5, 1.5)
    w_gate = noise(key_list[10], (D, FF), D ** -0.5, 0.125, ((1, 4),))
    w_up = noise(key_list[11], (D, FF), D ** -0.5, 0.125, ((1, 4),))
    w_down = noise(key_list[12], (FF, D), FF ** -0.5, 0.078125, ((0, 4),))
    return dict(inputs=inputs, teacher=teacher, lengths=lengths, gain_one=gain_one, w_query_down=w_query_down, gain_query=gain_query, w_query_up=w_query_up, w_keyvalue=w_keyvalue, w_output=w_output, gain_two=gain_two, w_gate=w_gate, w_up=w_up, w_down=w_down)


@jax.custom_vjp
def low(v):
    return lax.optimization_barrier(v.astype(jnp.bfloat16)).astype(jnp.float32)

@jax.custom_vjp
def low_back(v):
    return v

def low_keep(v):
    return (low(v), None)

def low_pass(kept, grad):
    return (grad,)

def back_keep(v):
    return (v, None)

def back_low(kept, grad):
    return (low(grad),)
low.defvjp(low_keep, low_pass)
low_back.defvjp(back_keep, back_low)
epsilon = 1e-05
masked_score = -1e+30
highest = lax.Precision.HIGHEST

def product(left, right):
    return jnp.dot(left, right, precision=highest, preferred_element_type=jnp.float32)

def rms_scale(values, gain):
    inverse = lax.rsqrt(lax.optimization_barrier(jnp.mean(values * values, axis=-1, keepdims=True)) + epsilon)
    return gain * values * inverse

def rope_angles(positions, pair_index, head_dim):
    frequency = jnp.exp(-math.log(10000.0) * (2.0 / head_dim) * pair_index)
    angles = positions[:, None] * frequency[None, :]
    return (jnp.cos(angles), jnp.sin(angles))

def rotate_pairs(values, cosines, sines):
    paired = values.reshape(values.shape[:-1] + (values.shape[-1] // 2, 2))
    even_part = paired[..., 0]
    odd_part = paired[..., 1]
    turned = jnp.stack([even_part * cosines - odd_part * sines, even_part * sines + odd_part * cosines], axis=-1)
    return turned.reshape(values.shape)

def layer_forward(params, inputs, length):
    gain_one, w_query_down, gain_query, w_query_up, w_keyvalue, w_output, gain_two, w_gate, w_up, w_down = params
    normed = low(rms_scale(inputs, gain_one))
    latent = low(low_back(product(normed, w_query_down)))
    latent_normed = low(rms_scale(latent, gain_query))
    query_pre = low_back(product(latent_normed, w_query_up)).reshape(LEN, HEADS, HD)
    keyvalue_pre = low_back(product(normed, w_keyvalue))
    positions = jnp.arange(LEN, dtype=jnp.float32)
    cosines, sines = rope_angles(positions, jnp.arange(HD // 2, dtype=jnp.float32), HD)
    query_rows = low(rotate_pairs(query_pre, cosines[:, None, :], sines[:, None, :]))
    key_rows = low(rotate_pairs(keyvalue_pre[:, :HD], cosines, sines))
    value_rows = low(keyvalue_pre[:, HD:])
    raw_scores = low_back(jnp.einsum('qhd,kd->hqk', query_rows, key_rows, precision=highest))
    index_rows = jnp.arange(LEN)
    allowed = (index_rows[:, None] >= index_rows[None, :]) & (index_rows[None, :] < length)
    scores = jnp.where(allowed[None], raw_scores * (1.0 / math.sqrt(HD)), masked_score)
    probability = low(jax.nn.softmax(scores, axis=-1))
    context = jnp.einsum('hqk,kd->qhd', probability, value_rows, precision=highest)
    context = low(low_back(context)).reshape(LEN, N_TENSOR, HEADS * HD // N_TENSOR)
    out_groups = w_output.reshape(N_TENSOR, HEADS * HD // N_TENSOR, D)
    partials = jnp.einsum('tgc,gcd->gtd', context, out_groups, precision=highest)
    residual = inputs + low_back(lax.optimization_barrier(jnp.sum(low(partials), axis=0)))
    normed_two = low(rms_scale(residual, gain_two))
    gate_values = low_back(product(normed_two, w_gate))
    up_values = low_back(product(normed_two, w_up))
    hidden = low(jax.nn.silu(gate_values) * up_values)
    return low(residual + low_back(product(hidden, w_down)))

def reference(inputs, teacher, lengths, gain_one, w_query_down, gain_query, w_query_up, w_keyvalue, w_output, gain_two, w_gate, w_up, w_down):
    params = tuple((weight.astype(jnp.float32) for weight in (gain_one, w_query_down, gain_query, w_query_up, w_keyvalue, w_output, gain_two, w_gate, w_up, w_down)))
    valid_count = jnp.sum(lengths).astype(jnp.float32)
    factor = jnp.float32(TOKENS) / valid_count
    seq_inputs = inputs.astype(jnp.float32).reshape(SEQS, LEN, D)
    seq_teacher = teacher.astype(jnp.float32).reshape(SEQS, LEN, D)

    def one_sequence(running, pieces):
        grad_totals, error_sum = running
        seq_in, seq_target, length = pieces

        def forward(weights, values):
            return layer_forward(weights, values, length)
        output, pullback = jax.vjp(forward, params, seq_in)
        valid_rows = (jnp.arange(LEN) < length)[:, None]
        differ = jnp.where(valid_rows, output - seq_target, jnp.float32(0.0))
        error_sum = error_sum + jnp.sum(differ * differ)
        weight_grads, input_grad = pullback(differ * factor)
        grad_totals = jax.tree.map(jnp.add, grad_totals, weight_grads)
        return ((grad_totals, error_sum), (output.astype(jnp.bfloat16), input_grad.astype(jnp.bfloat16)))
    empty_grads = jax.tree.map(jnp.zeros_like, params)
    (grad_totals, error_total), (outputs, input_grads) = lax.scan(one_sequence, (empty_grads, jnp.float32(0.0)), (seq_inputs, seq_teacher, lengths))
    layer_loss = error_total / (valid_count * D)
    grad_gain_one, grad_query_down, grad_gain_query, grad_query_up, grad_keyvalue, grad_output, grad_gain_two, grad_gate, grad_up, grad_down = grad_totals
    return (outputs.reshape(TOKENS, D), layer_loss, input_grads.reshape(TOKENS, D), grad_gain_one, grad_query_down, grad_gain_query, grad_query_up, grad_keyvalue, grad_output, grad_gain_two, grad_gate, grad_up, grad_down)
```

```python
import math

import jax
import jax.numpy as jnp
from jax import lax
from jax.sharding import PartitionSpec as P

epsilon = 1e-05
masked_score = -1e30


def rope_angles(positions, pair_index, head_dim):
    frequency = jnp.exp(-math.log(10000.0) * (2.0 / head_dim) * pair_index)
    angles = positions[:, None] * frequency[None, :]
    return (jnp.cos(angles), jnp.sin(angles))


def rotate_pairs(values, cosines, sines):
    paired = values.reshape(values.shape[:-1] + (values.shape[-1] // 2, 2))
    even_part = paired[..., 0]
    odd_part = paired[..., 1]
    turned = jnp.stack(
        [even_part * cosines - odd_part * sines, even_part * sines + odd_part * cosines], axis=-1
    )
    return turned.reshape(values.shape)


def spread_latent(latent_rows):
    return lax.all_gather(latent_rows, "tensor", axis=1, tiled=True)


def dp_layout():
    size = lax.axis_size("dp")
    depth = 4 if size % 4 == 0 else 1
    return depth, size // depth


def dp_permute(values, pairs):
    return lax.ppermute(values, "dp", pairs)


def chain_pairs(depth, width):
    def index(level, column):
        return level * width + column

    inward = [
        pair
        for column in range(width)
        for pair in (
            (index(0, column), index(1, column)),
            (index(depth - 1, column), index(depth - 2, column)),
        )
    ]
    middle = [
        pair
        for column in range(width)
        for pair in (
            (index(1, column), index(2, column)),
            (index(2, column), index(1, column)),
        )
    ]
    outward = [(target, source) for source, target in inward]
    return inward, middle, outward


def width_masks(width):
    masks = []
    mask = 1
    while mask < width:
        masks.append(mask)
        mask *= 2
    return masks


def swap_pairs(depth, width, mask, levels):
    return [
        (level * width + column, level * width + (column ^ mask))
        for level in levels
        for column in range(width)
    ]


def split_rows(values, bit):
    half = values.shape[0] // 2
    keep = lax.dynamic_slice_in_dim(values, bit * half, half, 0)
    send = lax.dynamic_slice_in_dim(values, (1 - bit) * half, half, 0)
    return keep, send


def join_rows(mine, theirs, bit):
    first = bit == 0
    return jnp.concatenate(
        [jnp.where(first, mine, theirs), jnp.where(first, theirs, mine)], axis=0
    )


def sum_columns_first(values):
    depth, width = dp_layout()
    index = lax.axis_index("dp")
    level, column = index // width, index % width
    inward, middle, outward = chain_pairs(depth, width)
    is_end = (level == 0) | (level == depth - 1)
    masks = width_masks(width)
    current = values
    for mask in masks:
        keep, send = split_rows(current, (column // mask) % 2)
        current = keep + dp_permute(send, swap_pairs(depth, width, mask, range(depth)))
    current = current + dp_permute(current, inward)
    current = current + dp_permute(current, middle)
    current = jnp.where(is_end, dp_permute(current, outward), current)
    for mask in reversed(masks):
        other = dp_permute(current, swap_pairs(depth, width, mask, range(depth)))
        current = join_rows(current, other, (column // mask) % 2)
    return current


def sum_levels_first(values):
    depth, width = dp_layout()
    index = lax.axis_index("dp")
    level = index // width
    inward, middle, outward = chain_pairs(depth, width)
    is_end = (level == 0) | (level == depth - 1)
    upper = (level >= depth // 2).astype(jnp.int32)
    current = values + dp_permute(values, inward)
    keep, send = split_rows(current, upper)
    current = keep + dp_permute(send, middle)
    for mask in width_masks(width):
        current = current + dp_permute(current, swap_pairs(depth, width, mask, (1, 2)))
    other = dp_permute(current, middle)
    mine = jnp.where(is_end, dp_permute(current, outward), current)
    theirs = jnp.where(is_end, dp_permute(other, outward), other)
    return join_rows(mine, theirs, upper)


def sum_over_dp(chunks):
    if dp_layout()[0] != 4:
        return [lax.psum(chunk, "dp") for chunk, _ in chunks]
    return [
        (sum_columns_first if kind == 0 else sum_levels_first)(chunk) for chunk, kind in chunks
    ]


def causal_mask(offset, block_rows, seq_len, key_live):
    query_pos = offset + jnp.arange(block_rows)
    causal = query_pos[:, None] >= jnp.arange(seq_len)[None, :]
    return causal[None, None] & key_live[:, None, None, :]


def local(
    inputs,
    teacher,
    lengths,
    gain_one,
    w_query_down,
    gain_query,
    w_query_up,
    w_keyvalue,
    w_output,
    gain_two,
    w_gate,
    w_up,
    w_down,
):
    groups = lax.axis_size("tensor")
    member = lax.axis_index("tensor")
    tokens, model_width = inputs.shape
    seq_count = lengths.shape[0]
    seq_len = tokens // seq_count
    head_dim = w_keyvalue.shape[1] // 2
    local_heads = w_query_up.shape[1] // head_dim
    rank_local = w_query_down.shape[1]
    rank_full = w_query_up.shape[0]
    width_local = model_width // groups
    keyvalue_local = 2 * head_dim // groups
    block_rows = min(512, seq_len)
    score_scale = 1.0 / math.sqrt(head_dim)
    positions = jnp.arange(seq_len, dtype=jnp.float32)
    cosines, sines = rope_angles(positions, jnp.arange(head_dim // 2, dtype=jnp.float32), head_dim)
    key_live = jnp.arange(seq_len)[None, :] < lengths[:, None]
    valid_rows = key_live.reshape(tokens, 1)
    inputs_f = inputs.astype(jnp.float32)
    inverse_one = lax.rsqrt(jnp.mean(inputs_f * inputs_f, axis=-1, keepdims=True) + epsilon)
    normed = (gain_one * inputs_f * inverse_one).astype(jnp.bfloat16)
    latent = jnp.dot(normed, w_query_down, preferred_element_type=jnp.float32).astype(jnp.bfloat16)
    latent_f = latent.astype(jnp.float32)
    gain_slice = lax.dynamic_slice_in_dim(gain_query, member * rank_local, rank_local)
    squares = lax.psum(jnp.sum(latent_f * latent_f, axis=-1), "tensor")
    inverse_query = lax.rsqrt(squares / rank_full + epsilon)[:, None]
    latent_normed = spread_latent((gain_slice * latent_f * inverse_query).astype(jnp.bfloat16))
    query_pre = jnp.dot(latent_normed, w_query_up, preferred_element_type=jnp.float32)
    query_rows = rotate_pairs(
        query_pre.reshape(seq_count, seq_len, local_heads, head_dim),
        cosines[None, :, None, :],
        sines[None, :, None, :],
    ).astype(jnp.bfloat16)
    keyvalue_pre = jnp.dot(normed, w_keyvalue, preferred_element_type=jnp.float32).reshape(
        seq_count, seq_len, 2 * head_dim
    )
    key_rows = rotate_pairs(keyvalue_pre[..., :head_dim], cosines[None], sines[None]).astype(
        jnp.bfloat16
    )
    value_rows = keyvalue_pre[..., head_dim:].astype(jnp.bfloat16)
    contexts = []
    log_totals = []
    for offset in range(0, seq_len, block_rows):
        query_block = query_rows[:, offset : offset + block_rows]
        allowed = causal_mask(offset, block_rows, seq_len, key_live)
        scores = (
            jnp.einsum("sqhd,skd->shqk", query_block, key_rows, preferred_element_type=jnp.float32)
            * score_scale
        )
        scores = jnp.where(allowed, scores, masked_score)
        row_peak = jnp.max(scores, axis=-1, keepdims=True)
        weights = jnp.exp(scores - row_peak)
        totals = jnp.sum(weights, axis=-1, keepdims=True)
        probability = (weights / totals).astype(jnp.bfloat16)
        log_totals.append(row_peak + jnp.log(totals))
        contexts.append(
            jnp.einsum(
                "shqk,skd->sqhd", probability, value_rows, preferred_element_type=jnp.float32
            )
        )
    context = (
        jnp.concatenate(contexts, axis=1)
        .reshape(tokens, local_heads * head_dim)
        .astype(jnp.bfloat16)
    )
    attention_sum = lax.psum(
        jnp.dot(context, w_output, preferred_element_type=jnp.float32).astype(jnp.bfloat16),
        "tensor",
    ).astype(jnp.float32)
    residual = inputs_f + attention_sum
    inverse_two = lax.rsqrt(jnp.mean(residual * residual, axis=-1, keepdims=True) + epsilon)
    normed_two = (gain_two * residual * inverse_two).astype(jnp.bfloat16)
    gate_values = jnp.dot(normed_two, w_gate, preferred_element_type=jnp.float32)
    up_values = jnp.dot(normed_two, w_up, preferred_element_type=jnp.float32)
    sigmoid_gate = jax.nn.sigmoid(gate_values)
    silu_gate = gate_values * sigmoid_gate
    hidden = (silu_gate * up_values).astype(jnp.bfloat16)
    feed_share = lax.psum_scatter(
        jnp.dot(hidden, w_down, preferred_element_type=jnp.float32).astype(jnp.bfloat16),
        "tensor",
        scatter_dimension=1,
        tiled=True,
    ).astype(jnp.float32)
    residual_share = lax.dynamic_slice_in_dim(residual, member * width_local, width_local, 1)
    output = (residual_share + feed_share).astype(jnp.bfloat16)
    differ = jnp.where(valid_rows, output.astype(jnp.float32) - teacher.astype(jnp.float32), 0.0)
    error_sum, valid_count = lax.psum(
        (jnp.sum(differ * differ), jnp.sum(lengths).astype(jnp.float32) / groups), ("dp", "tensor")
    )
    layer_loss = error_sum / (valid_count * model_width)
    grad_scale = float(tokens * lax.axis_size("dp")) / valid_count
    grad_out = lax.all_gather(differ.astype(jnp.bfloat16), "tensor", axis=1, tiled=True).astype(
        jnp.float32
    )
    grad_out_low = grad_out.astype(jnp.bfloat16)
    grad_w_down = jnp.einsum("tf,td->fd", hidden, grad_out_low, preferred_element_type=jnp.float32)
    grad_hidden = jnp.einsum("td,fd->tf", grad_out_low, w_down, preferred_element_type=jnp.float32)
    gate_grad = (
        grad_hidden * up_values * sigmoid_gate * (1.0 + gate_values * (1.0 - sigmoid_gate))
    ).astype(jnp.bfloat16)
    up_grad = (grad_hidden * silu_gate).astype(jnp.bfloat16)
    grad_w_gate = jnp.einsum("tk,tf->kf", normed_two, gate_grad, preferred_element_type=jnp.float32)
    grad_w_up = jnp.einsum("tk,tf->kf", normed_two, up_grad, preferred_element_type=jnp.float32)
    normed_two_part = jnp.einsum(
        "tf,kf->tk", gate_grad, w_gate, preferred_element_type=jnp.float32
    ) + jnp.einsum("tf,kf->tk", up_grad, w_up, preferred_element_type=jnp.float32)
    grad_normed_two = lax.psum(normed_two_part.astype(jnp.bfloat16), "tensor").astype(jnp.float32)
    scaled_two = gain_two * grad_normed_two
    grad_residual = (
        grad_out
        + inverse_two * scaled_two
        - residual * inverse_two**3 * jnp.mean(scaled_two * residual, axis=-1, keepdims=True)
    )
    grad_gain_two = lax.dynamic_slice_in_dim(
        jnp.sum(grad_normed_two * residual * inverse_two, axis=0), member * width_local, width_local
    )
    grad_residual_low = grad_residual.astype(jnp.bfloat16)
    residual_grad_share = lax.dynamic_slice_in_dim(
        grad_residual, member * width_local, width_local, 1
    )
    grad_w_output = jnp.einsum(
        "tc,td->cd", context, grad_residual_low, preferred_element_type=jnp.float32
    )
    grad_context = jnp.einsum(
        "td,cd->tc", grad_residual_low, w_output, preferred_element_type=jnp.float32
    ).astype(jnp.bfloat16)
    grad_context = grad_context.reshape(seq_count, seq_len, local_heads, head_dim)
    grad_keys = jnp.zeros((seq_count, seq_len, head_dim), jnp.float32)
    grad_values = jnp.zeros((seq_count, seq_len, head_dim), jnp.float32)
    grad_queries = []
    for number, offset in enumerate(range(0, seq_len, block_rows)):
        query_block = query_rows[:, offset : offset + block_rows]
        allowed = causal_mask(offset, block_rows, seq_len, key_live)
        scores = (
            jnp.einsum("sqhd,skd->shqk", query_block, key_rows, preferred_element_type=jnp.float32)
            * score_scale
        )
        scores = jnp.where(allowed, scores, masked_score)
        probability = jnp.where(allowed, jnp.exp(scores - log_totals[number]), 0.0)
        grad_block = grad_context[:, offset : offset + block_rows]
        grad_probs = jnp.einsum(
            "sqhd,skd->shqk", grad_block, value_rows, preferred_element_type=jnp.float32
        )
        inner = jnp.sum(probability * grad_probs, axis=-1, keepdims=True)
        grad_scores = (score_scale * probability * (grad_probs - inner)).astype(jnp.bfloat16)
        grad_queries.append(
            jnp.einsum("shqk,skd->sqhd", grad_scores, key_rows, preferred_element_type=jnp.float32)
        )
        grad_keys = grad_keys + jnp.einsum(
            "shqk,sqhd->skd", grad_scores, query_block, preferred_element_type=jnp.float32
        )
        grad_values = grad_values + jnp.einsum(
            "shqk,sqhd->skd",
            probability.astype(jnp.bfloat16),
            grad_block,
            preferred_element_type=jnp.float32,
        )
    grad_query_rows = jnp.concatenate(grad_queries, axis=1)
    grad_query_pre = (
        rotate_pairs(grad_query_rows, cosines[None, :, None, :], -sines[None, :, None, :])
        .reshape(tokens, local_heads * head_dim)
        .astype(jnp.bfloat16)
    )
    grad_w_query_up = jnp.einsum(
        "tr,tc->rc", latent_normed, grad_query_pre, preferred_element_type=jnp.float32
    )
    keyvalue_part = jnp.concatenate([grad_keys, grad_values], axis=-1).reshape(tokens, 2 * head_dim)
    latent_part = jnp.einsum(
        "tc,rc->tr", grad_query_pre, w_query_up, preferred_element_type=jnp.float32
    )
    keyvalue_share, latent_share = (
        lax.psum_scatter(
            keyvalue_part.astype(jnp.bfloat16), "tensor", scatter_dimension=1, tiled=True
        ).astype(jnp.float32),
        lax.psum_scatter(
            latent_part.astype(jnp.bfloat16), "tensor", scatter_dimension=1, tiled=True
        ).astype(jnp.float32),
    )
    pair_global = member * (keyvalue_local // 2) + jnp.arange(keyvalue_local // 2)
    pair_keys = pair_global < head_dim // 2
    slice_cos, slice_sin = rope_angles(
        positions, (pair_global % (head_dim // 2)).astype(jnp.float32), head_dim
    )
    keyvalue_seq = keyvalue_share.reshape(seq_count, seq_len, keyvalue_local)
    turned = rotate_pairs(keyvalue_seq, slice_cos[None], -slice_sin[None])
    grad_keyvalue = (
        jnp.where(jnp.repeat(pair_keys, 2)[None, None, :], turned, keyvalue_seq)
        .reshape(tokens, keyvalue_local)
        .astype(jnp.bfloat16)
    )
    w_keyvalue_share = lax.dynamic_slice_in_dim(
        w_keyvalue, member * keyvalue_local, keyvalue_local, 1
    )
    grad_w_keyvalue = jnp.einsum(
        "tk,tc->kc", normed, grad_keyvalue, preferred_element_type=jnp.float32
    )
    scaled_latent = gain_slice * latent_share
    grad_gain_query = jnp.sum(latent_share * latent_f * inverse_query, axis=0)
    latent_dots = lax.psum(jnp.sum(scaled_latent * latent_f, axis=-1), "tensor")
    grad_latent = (
        inverse_query * scaled_latent
        - latent_f * inverse_query**3 * (latent_dots / rank_full)[:, None]
    ).astype(jnp.bfloat16)
    grad_w_query_down = jnp.einsum(
        "tk,tr->kr", normed, grad_latent, preferred_element_type=jnp.float32
    )
    normed_part = jnp.einsum(
        "tr,kr->tk", grad_latent, w_query_down, preferred_element_type=jnp.float32
    ) + jnp.einsum("tc,kc->tk", grad_keyvalue, w_keyvalue_share, preferred_element_type=jnp.float32)
    grad_normed = lax.psum_scatter(
        normed_part.astype(jnp.bfloat16), "tensor", scatter_dimension=1, tiled=True
    ).astype(jnp.float32)
    inputs_share = lax.dynamic_slice_in_dim(inputs_f, member * width_local, width_local, 1)
    gain_share = lax.dynamic_slice_in_dim(gain_one, member * width_local, width_local)
    scaled_one = gain_share * grad_normed
    input_dots = lax.psum(jnp.sum(scaled_one * inputs_share, axis=-1), "tensor")
    grad_gain_one = jnp.sum(grad_normed * inputs_share * inverse_one, axis=0)
    input_grad = (
        grad_scale
        * (
            residual_grad_share
            + inverse_one * scaled_one
            - inputs_share * inverse_one**3 * (input_dots / model_width)[:, None]
        )
    ).astype(jnp.bfloat16)
    grad_gains = lax.psum(
        jnp.concatenate([grad_gain_one, grad_gain_query, grad_gain_two]), "dp"
    )
    grad_gain_one, grad_gain_query, grad_gain_two = jnp.split(
        grad_gains * grad_scale, [width_local, width_local + rank_local]
    )
    weight_grads = {}
    for name, values in (
        ("down", grad_w_down),
        ("gate", grad_w_gate),
        ("up", grad_w_up),
        ("output", grad_w_output),
        ("query_up", grad_w_query_up),
        ("query_down", grad_w_query_down),
        ("keyvalue", grad_w_keyvalue),
    ):
        low = values.astype(jnp.bfloat16)
        half = low.shape[0] // 2
        if name == "keyvalue":
            totals = sum_over_dp([(low, 0)])
        elif name == "query_down":
            totals = sum_over_dp([(low, 1)])
        else:
            totals = sum_over_dp([(low[:half], 0), (low[half:], 1)])
        weight_grads[name] = jnp.concatenate(totals, axis=0).astype(jnp.float32) * grad_scale
    grad_w_down, grad_w_gate, grad_w_up, grad_w_output = (
        weight_grads[name] for name in ("down", "gate", "up", "output")
    )
    grad_w_query_up, grad_w_query_down, grad_w_keyvalue = (
        weight_grads[name] for name in ("query_up", "query_down", "keyvalue")
    )
    return (
        output,
        layer_loss,
        input_grad,
        grad_gain_one,
        grad_w_query_down,
        grad_gain_query,
        grad_w_query_up,
        grad_w_keyvalue,
        grad_w_output,
        grad_gain_two,
        grad_w_gate,
        grad_w_up,
        grad_w_down,
    )


def solution(mesh):
    placed = (
        P("dp", None),
        P("dp", "tensor"),
        P("dp"),
        P(),
        P(None, "tensor"),
        P(),
        P(None, "tensor"),
        P(),
        P("tensor", None),
        P(),
        P(None, "tensor"),
        P(None, "tensor"),
        P("tensor", None),
    )
    return jax.shard_map(
        local,
        mesh=mesh,
        in_specs=placed,
        out_specs=(
            P("dp", "tensor"),
            P(),
            P("dp", "tensor"),
            P("tensor"),
            P(None, "tensor"),
            P("tensor"),
            P(None, "tensor"),
            P(None, "tensor"),
            P("tensor", None),
            P("tensor"),
            P(None, "tensor"),
            P(None, "tensor"),
            P("tensor", None),
        ),
        check_vma=False,
    )
```

```python
import functools
import math

import jax
import jax.numpy as jnp
from jax import lax
from jax.experimental import pallas as pl
from jax.experimental.pallas import tpu as pltpu
from jax.sharding import PartitionSpec as P


epsilon = 1e-05
masked_score = -1e30


def rope_angles(positions, pair_index, head_dim):
    frequency = jnp.exp(-math.log(10000.0) * (2.0 / head_dim) * pair_index)
    angles = positions[:, None] * frequency[None, :]
    return (jnp.cos(angles), jnp.sin(angles))


def dp_layout():
    size = lax.axis_size("dp")
    depth = 4 if size % 4 == 0 else 1
    return depth, size // depth


def split_rows(values, bit):
    half = values.shape[0] // 2
    keep = lax.dynamic_slice_in_dim(values, bit * half, half, 0)
    send = lax.dynamic_slice_in_dim(values, (1 - bit) * half, half, 0)
    return keep, send


def join_rows(mine, theirs, bit):
    first = bit == 0
    return jnp.concatenate(
        [jnp.where(first, mine, theirs), jnp.where(first, theirs, mine)], axis=0
    )


chunk_rows = 64
slots = 8


def grid_place(width):
    index = lax.axis_index("dp")
    level, column = index // width, index % width
    is_end = (level == 0) | (level == 3)
    upper = level // 2
    column_partner = level * width + (1 - column)
    chain_level = jnp.where(is_end, 1 + upper, 3 * upper)
    chain_partner = chain_level * width + column
    middle_partner = (3 - level) * width + column
    return column, upper, is_end, column_partner, chain_partner, middle_partner


def sum_kernel(starts, width, *refs):
    count = len(starts) - 1
    sources, results = refs[:count], refs[count : 2 * count]
    (
        load_a, first_a, sum_a, second_a, third_a, total_a, other_a,
        load_b, first_b, sum_b, second_b, half_b, third_b, total_b, other_b,
        load_sem, store_sem, send_sem, recv_sem,
    ) = refs[2 * count :]
    rounds = starts[-1] // 2
    half = chunk_rows // 2
    column, upper, is_end, column_partner, chain_partner, middle_partner = grid_place(width)
    is_middle = jnp.logical_not(is_end)

    def signal(partner):
        pl.semaphore_signal(
            barrier, inc=1, device_id={"dp": partner}, device_id_type=pl.DeviceIdType.MESH
        )

    barrier = pltpu.get_barrier_semaphore()
    signal(column_partner)
    signal(chain_partner)

    @pl.when(is_middle)
    def _():
        signal(middle_partner)

    pl.semaphore_wait(barrier, jnp.where(is_end, 2, 3))

    def remote(kind, slot, source, target, partner):
        return pltpu.make_async_remote_copy(
            src_ref=source,
            dst_ref=target,
            send_sem=send_sem.at[kind, slot],
            recv_sem=recv_sem.at[kind, slot],
            device_id={"dp": partner},
            device_id_type=pl.DeviceIdType.MESH,
        )

    def load(kind, number, slot, target):
        chunk = 2 * number + kind
        for i in range(count):

            @pl.when((chunk >= starts[i]) & (chunk < starts[i + 1]))
            def _():
                row = pl.multiple_of((chunk - starts[i]) * chunk_rows, chunk_rows)
                pltpu.make_async_copy(
                    sources[i].at[pl.ds(row, chunk_rows)], target.at[slot], load_sem.at[kind, slot]
                ).start()

    def load_wait(kind, slot, target):
        pltpu.make_async_copy(
            sources[0].at[pl.ds(0, chunk_rows)], target.at[slot], load_sem.at[kind, slot]
        ).wait()

    def store(kind, number, slot, bit, mine, theirs):
        chunk = 2 * number + kind
        for i in range(count):

            @pl.when((chunk >= starts[i]) & (chunk < starts[i + 1]))
            def _():
                row = (chunk - starts[i]) * chunk_rows
                for part, (ref, side) in enumerate(((mine, bit), (theirs, 1 - bit))):
                    place = pl.multiple_of(row + side * half, half)
                    pltpu.make_async_copy(
                        ref.at[slot], results[i].at[pl.ds(place, half)], store_sem.at[kind, part, slot]
                    ).start()

    def store_wait(kind, slot, mine, theirs):
        for part, ref in enumerate((mine, theirs)):
            pltpu.make_async_copy(
                ref.at[slot], results[0].at[pl.ds(0, half)], store_sem.at[kind, part, slot]
            ).wait()

    def rows(side):
        return pl.ds(pl.multiple_of(side * half, half), half)

    def plus(left, right):
        return (left.astype(jnp.float32) + right.astype(jnp.float32)).astype(jnp.bfloat16)

    def copy_a1(slot):
        return remote(0, slot, load_a.at[slot, rows(1 - column)], first_a.at[slot], column_partner)

    def copy_a2(slot):
        return remote(1, slot, sum_a.at[slot], second_a.at[slot], chain_partner)

    def copy_a3(slot):
        return remote(2, slot, sum_a.at[slot], third_a.at[slot], middle_partner)

    def copy_a4(slot):
        return remote(3, slot, total_a.at[slot], total_a.at[slot], chain_partner)

    def copy_a5(slot):
        return remote(4, slot, total_a.at[slot], other_a.at[slot], column_partner)

    def copy_b1(slot):
        return remote(5, slot, load_b.at[slot], first_b.at[slot], chain_partner)

    def copy_b2(slot):
        return remote(6, slot, sum_b.at[slot, rows(1 - upper)], second_b.at[slot], middle_partner)

    def copy_b3(slot):
        return remote(7, slot, half_b.at[slot], third_b.at[slot], column_partner)

    def copy_b4(slot):
        return remote(8, slot, total_b.at[slot], other_b.at[slot], middle_partner)

    def copy_b5(slot):
        return remote(9, slot, total_b.at[slot], total_b.at[slot], chain_partner)

    def copy_b6(slot):
        return remote(10, slot, other_b.at[slot], other_b.at[slot], chain_partner)

    def stage(number, body):
        @pl.when((number >= 0) & (number < rounds))
        def _():
            body(number, lax.rem(number + slots, slots))

    def stage_6(number, slot):
        store_wait(0, slot, total_a, other_a)
        store_wait(1, slot, total_b, other_b)

    def stage_5(number, slot):
        copy_a5(slot).wait_recv()
        copy_a1(slot).wait_send()
        copy_a5(slot).wait_send()

        @pl.when(is_end)
        def _():
            copy_b5(slot).wait_recv()
            copy_b6(slot).wait_recv()
            copy_a2(slot).wait_send()
            copy_b1(slot).wait_send()

        @pl.when(is_middle)
        def _():
            copy_a3(slot).wait_send()
            copy_a4(slot).wait_send()
            copy_b2(slot).wait_send()
            copy_b3(slot).wait_send()
            copy_b4(slot).wait_send()
            copy_b5(slot).wait_send()
            copy_b6(slot).wait_send()

        store(0, number, slot, column, total_a, other_a)
        store(1, number, slot, upper, total_b, other_b)

    def stage_4(number, slot):
        @pl.when(is_end)
        def _():
            copy_a4(slot).wait_recv()
            copy_a5(slot).start()

        @pl.when(is_middle)
        def _():
            copy_b4(slot).wait_recv()
            copy_b6(slot).start()

    def stage_3(number, slot):
        @pl.when(is_middle)
        def _():
            copy_a3(slot).wait_recv()
            total_a[slot] = plus(sum_a[slot], third_a[slot])
            copy_a4(slot).start()
            copy_a5(slot).start()
            copy_b3(slot).wait_recv()
            total_b[slot] = plus(half_b[slot], third_b[slot])
            copy_b4(slot).start()
            copy_b5(slot).start()

    def stage_2(number, slot):
        @pl.when(is_middle)
        def _():
            copy_a2(slot).wait_recv()
            sum_a[slot] = plus(sum_a[slot], second_a[slot])
            copy_a3(slot).start()
            copy_b2(slot).wait_recv()
            half_b[slot] = plus(sum_b[slot, rows(upper)], second_b[slot])
            copy_b3(slot).start()

    def stage_1(number, slot):
        copy_a1(slot).wait_recv()
        sum_a[slot] = plus(load_a[slot, rows(column)], first_a[slot])

        @pl.when(is_end)
        def _():
            copy_a2(slot).start()

        @pl.when(is_middle)
        def _():
            copy_b1(slot).wait_recv()
            sum_b[slot] = plus(load_b[slot], first_b[slot])
            copy_b2(slot).start()

    def stage_0(number, slot):
        load_wait(0, slot, load_a)
        copy_a1(slot).start()
        load_wait(1, slot, load_b)

        @pl.when(is_end)
        def _():
            copy_b1(slot).start()

    def prefetch(number, slot):
        load(0, number, slot, load_a)
        load(1, number, slot, load_b)

    prefetch(0, 0)
    stages = (stage_0, stage_1, stage_2, stage_3, stage_4, stage_5, stage_6)

    def step(number, carry):
        for late in range(len(stages) - 1, -1, -1):
            stage(number - late, stages[late])
        stage(number + 1, prefetch)
        return carry

    lax.fori_loop(0, rounds + len(stages) - 1, step, 0)


def kernel_sum(arrays):
    width = dp_layout()[1]
    starts = [0]
    for values in arrays:
        starts.append(starts[-1] + values.shape[0] // chunk_rows)
    columns = arrays[0].shape[1]
    half = chunk_rows // 2
    full_slot = pltpu.VMEM((slots, chunk_rows, columns), jnp.bfloat16)
    half_slot = pltpu.VMEM((slots, half, columns), jnp.bfloat16)
    moved = sum(values.size for values in arrays) * 2
    return pl.pallas_call(
        functools.partial(sum_kernel, tuple(starts), width),
        out_shape=[jax.ShapeDtypeStruct(values.shape, values.dtype) for values in arrays],
        in_specs=[pl.BlockSpec(memory_space=pl.ANY)] * len(arrays),
        out_specs=[pl.BlockSpec(memory_space=pl.ANY)] * len(arrays),
        scratch_shapes=[
            full_slot, half_slot, half_slot, half_slot, half_slot, half_slot, half_slot,
            full_slot, full_slot, full_slot, half_slot, half_slot, half_slot, half_slot, half_slot,
            pltpu.SemaphoreType.DMA((2, slots)),
            pltpu.SemaphoreType.DMA((2, 2, slots)),
            pltpu.SemaphoreType.DMA((11, slots)),
            pltpu.SemaphoreType.DMA((11, slots)),
        ],
        compiler_params=pltpu.CompilerParams(
            collective_id=0, has_side_effects=True, vmem_limit_bytes=48 * 1024 * 1024
        ),
        cost_estimate=pl.CostEstimate(flops=moved, bytes_accessed=20 * moved, transcendentals=0),
    )(*arrays)


def transpose_kernel(scale_ref, values_ref, result_ref):
    result_ref[...] = values_ref[...].astype(jnp.float32).T * scale_ref[0]


def transpose_scaled(values, scale):
    rows, columns = values.shape
    return pl.pallas_call(
        transpose_kernel,
        grid=(rows // 128,),
        in_specs=[
            pl.BlockSpec(memory_space=pltpu.SMEM),
            pl.BlockSpec((128, columns), lambda i: (i, 0)),
        ],
        out_specs=pl.BlockSpec((columns, 128), lambda i: (0, i)),
        out_shape=jax.ShapeDtypeStruct((columns, rows), jnp.float32),
        cost_estimate=pl.CostEstimate(
            flops=values.size, bytes_accessed=6 * values.size, transcendentals=0
        ),
    )(scale.reshape(1), values)


def sum_over_dp(arrays):
    depth, width = dp_layout()
    rows = [values.shape[0] for values in arrays]
    even = sum(rows) % (2 * chunk_rows) == 0 and all(row % chunk_rows == 0 for row in rows)
    if (depth, width) == (4, 2) and even:
        return kernel_sum(arrays)
    return [lax.psum(values, "dp") for values in arrays]


def tensor_masks():
    size = lax.axis_size("tensor")
    masks = []
    mask = 1
    while mask < size:
        masks.append(mask)
        mask *= 2
    return masks


def tensor_permute(values, mask):
    size = lax.axis_size("tensor")
    return lax.ppermute(values, "tensor", [(i, i ^ mask) for i in range(size)])


def sum_over_tensor(values):
    core = lax.axis_index("tensor") % 2
    keep, send = split_rows(values, core)
    total = keep + tensor_permute(send, 1)
    for mask in tensor_masks()[1:]:
        received = tensor_permute(total, mask)
        total = total + received
    return join_rows(total, tensor_permute(total, 1), core)


def scatter_step(pieces, mask):
    high = (lax.axis_index("tensor") // mask) % 2 == 1
    lower, upper = pieces[0::2], pieces[1::2]
    keep = jnp.where(high, jnp.concatenate(upper, axis=1), jnp.concatenate(lower, axis=1))
    send = jnp.where(high, jnp.concatenate(lower, axis=1), jnp.concatenate(upper, axis=1))
    received = tensor_permute(send, mask)
    return jnp.split(keep + received, len(lower), axis=1)


def scatter_over_tensor(values):
    pieces = jnp.split(values, lax.axis_size("tensor"), axis=1)
    for mask in tensor_masks():
        pieces = scatter_step(pieces, mask)
    return pieces[0]


def gather_over_tensor(values):
    member = lax.axis_index("tensor")
    pieces = [values]
    for mask in reversed(tensor_masks()):
        low = (member // mask) % 2 == 0
        joined = jnp.concatenate(pieces, axis=1) if len(pieces) > 1 else pieces[0]
        received = tensor_permute(joined, mask)
        others = jnp.split(received, len(pieces), axis=1)
        pieces = [
            piece
            for own, other in zip(pieces, others)
            for piece in (jnp.where(low, own, other), jnp.where(low, other, own))
        ]
    return jnp.concatenate(pieces, axis=1)


def sum_small(values):
    flat = jnp.concatenate([value.reshape(-1) for value in values])
    size = flat.shape[0]
    total = jnp.pad(flat, (0, -size % 1024)).reshape(-1, 128)
    for mask in tensor_masks():
        total = total + tensor_permute(total, mask)
    ends = []
    for value in values:
        ends.append((ends[-1] if ends else 0) + value.size)
    return jnp.split(total.reshape(-1)[:size], ends[:-1])


def fold_rows(values, columns):
    return jnp.concatenate(jnp.split(values, columns // values.shape[1], axis=0), axis=1)


def unfold_rows(values, columns):
    return jnp.concatenate(jnp.split(values, values.shape[1] // columns, axis=1), axis=0)


def exact_parts(value, count):
    parts = []
    for _ in range(count):
        part = value.astype(jnp.bfloat16).astype(jnp.float32)
        parts.append(part)
        value = value - part
    return parts


def lane_angles(seq_len, head_dim):
    lane = jnp.arange(head_dim)
    cosines, sines = rope_angles(
        jnp.arange(seq_len, dtype=jnp.float32), (lane // 2).astype(jnp.float32), head_dim
    )
    return cosines, jnp.where(lane % 2 == 0, -sines, sines)


def turn_lanes(values, cosines, signed_sines):
    size = values.shape[1]
    even = lax.broadcasted_iota(jnp.int32, values.shape, 1) % 2 == 0
    partner = jnp.where(even, pltpu.roll(values, size - 1, 1), pltpu.roll(values, 1, 1))
    return values * cosines + partner * signed_sines


def across(left, right, left_dim, right_dim):
    return lax.dot_general(
        left,
        right,
        (((left_dim,), (right_dim,)), ((), ())),
        preferred_element_type=jnp.float32,
    )


def keyvalue_kernel(normed_ref, weight_ref, cos_ref, sin_ref, key_ref, value_ref):
    head_dim = key_ref.shape[1]
    both = across(normed_ref[...], weight_ref[...], 1, 0)
    key_ref[...] = turn_lanes(both[:, :head_dim], cos_ref[...], sin_ref[...]).astype(jnp.bfloat16)
    value_ref[...] = both[:, head_dim:].astype(jnp.bfloat16)


def softmax_block(query, key, length, offset, scale):
    scores = across(query, key, 1, 1) * scale
    row = offset + lax.broadcasted_iota(jnp.int32, scores.shape, 0)
    col = lax.broadcasted_iota(jnp.int32, scores.shape, 1)
    scores = jnp.where((row >= col) & (col < length), scores, masked_score)
    weights = jnp.exp(scores - jnp.max(scores, axis=1, keepdims=True))
    return weights * (1.0 / jnp.sum(weights, axis=1, keepdims=True))


def forward_kernel(
    offset, scale, length_ref, latent_ref, weight_ref, key_ref, value_ref, cos_ref, sin_ref,
    query_ref, context_ref,
):
    query = turn_lanes(
        across(latent_ref[...], weight_ref[...], 1, 0), cos_ref[...], sin_ref[...]
    ).astype(jnp.bfloat16)
    query_ref[...] = query
    probability = softmax_block(query, key_ref[...], length_ref[0], offset, scale)
    context_ref[...] = across(probability.astype(jnp.bfloat16), value_ref[...], 1, 0).astype(
        jnp.bfloat16
    )


def backward_kernel(
    offset, scale, final, length_ref, query_ref, grad_ref, key_ref, value_ref, cos_ref, sin_ref,
    key_cos_ref, key_sin_ref, *refs,
):
    earlier, (query_grad_ref, sums_ref, total) = refs[:-3], refs[-3:]
    size = query_ref.shape[1]
    head = pl.program_id(0)

    @pl.when(head == 0)
    def _():
        total[...] = jnp.zeros_like(total)
        if earlier:
            total[:offset] = earlier[0][...]

    query, key = query_ref[...], key_ref[...]
    probability = softmax_block(query, key, length_ref[0], offset, scale)
    grad_probs = across(grad_ref[...], value_ref[...], 1, 1)
    inner = jnp.sum(probability * grad_probs, axis=1, keepdims=True)
    grad_scores = (scale * probability * (grad_probs - inner)).astype(jnp.bfloat16)
    query_grad_ref[...] = turn_lanes(
        across(grad_scores, key, 1, 0), cos_ref[...], -sin_ref[...]
    ).astype(jnp.bfloat16)
    total[:, :size] += across(grad_scores, query, 0, 0)
    total[:, size:] += across(probability.astype(jnp.bfloat16), grad_ref[...], 0, 0)

    @pl.when(head == pl.num_programs(0) - 1)
    def _():
        if final:
            sums_ref[:, :size] = turn_lanes(
                total[:, :size], key_cos_ref[...], -key_sin_ref[...]
            ).astype(sums_ref.dtype)
            sums_ref[:, size:] = total[:, size:].astype(sums_ref.dtype)
        else:
            sums_ref[...] = total[...]


def project_keyvalue(normed, weight, cosines, sines):
    rows, width = normed.shape
    head_dim = weight.shape[1] // 2
    block = min(256, rows)
    angle = pl.BlockSpec((block, head_dim), lambda i: (i, 0))
    return pl.pallas_call(
        keyvalue_kernel,
        grid=(rows // block,),
        in_specs=[
            pl.BlockSpec((block, width), lambda i: (i, 0)),
            pl.BlockSpec(weight.shape, lambda i: (0, 0)),
            angle,
            angle,
        ],
        out_specs=[angle, angle],
        out_shape=[jax.ShapeDtypeStruct((rows, head_dim), jnp.bfloat16)] * 2,
        cost_estimate=pl.CostEstimate(
            flops=2 * normed.size * weight.shape[1], bytes_accessed=8 << 20, transcendentals=0
        ),
    )(normed, weight, cosines, sines)


def attend(part, block, length, latent, weight, key, value, cosines, sines):
    head_dim = key.shape[1]
    rank, columns = weight.shape
    live = (part + 1) * block
    head = pl.BlockSpec((block, head_dim), lambda h: (0, h))
    fixed = pl.BlockSpec((live, head_dim), lambda h: (0, 0))
    angle = pl.BlockSpec((block, head_dim), lambda h: (part, 0))
    return pl.pallas_call(
        functools.partial(forward_kernel, part * block, 1.0 / math.sqrt(head_dim)),
        grid=(columns // head_dim,),
        in_specs=[
            pl.BlockSpec(memory_space=pltpu.SMEM),
            pl.BlockSpec((block, rank), lambda h: (part, 0)),
            pl.BlockSpec((rank, head_dim), lambda h: (0, h)),
            fixed,
            fixed,
            angle,
            angle,
        ],
        out_specs=[head, head],
        out_shape=[jax.ShapeDtypeStruct((block, columns), jnp.bfloat16)] * 2,
        cost_estimate=pl.CostEstimate(
            flops=2 * block * columns * (rank + 2 * live),
            bytes_accessed=8 << 20,
            transcendentals=block * live * columns // head_dim,
        ),
    )(length, latent, weight, key, value, cosines, sines)


def attend_back(part, block, final, length, query, grad, key, value, cosines, sines, earlier):
    head_dim = key.shape[1]
    columns = query.shape[1]
    live = (part + 1) * block
    head = pl.BlockSpec((block, head_dim), lambda h: (0, h))
    fixed = pl.BlockSpec((live, head_dim), lambda h: (0, 0))
    angle = pl.BlockSpec((block, head_dim), lambda h: (part, 0))
    both = pl.BlockSpec((live, 2 * head_dim), lambda h: (0, 0))
    specs = [pl.BlockSpec(memory_space=pltpu.SMEM), head, head, fixed, fixed, angle, angle]
    specs += [fixed, fixed] + [pl.BlockSpec(values.shape, lambda h: (0, 0)) for values in earlier]
    return pl.pallas_call(
        functools.partial(backward_kernel, part * block, 1.0 / math.sqrt(head_dim), final),
        grid=(columns // head_dim,),
        in_specs=specs,
        out_specs=[head, both],
        out_shape=[
            jax.ShapeDtypeStruct((block, columns), jnp.bfloat16),
            jax.ShapeDtypeStruct(
                (live, 2 * head_dim), jnp.bfloat16 if final else jnp.float32
            ),
        ],
        scratch_shapes=[pltpu.VMEM((live, 2 * head_dim), jnp.float32)],
        cost_estimate=pl.CostEstimate(
            flops=10 * block * columns * live,
            bytes_accessed=8 << 20,
            transcendentals=block * live * columns // head_dim,
        ),
    )(length, query, grad, key, value, cosines, sines, cosines, sines, *earlier)


def layer(
    inputs,
    teacher,
    lengths,
    gain_one,
    w_query_down,
    gain_query,
    w_query_up,
    w_keyvalue,
    w_output,
    gain_two,
    w_gate,
    w_up,
    w_down,
):
    groups = lax.axis_size("tensor")
    member = lax.axis_index("tensor")
    tokens, model_width = inputs.shape
    seq_count = lengths.shape[0]
    seq_len = tokens // seq_count
    head_dim = w_keyvalue.shape[1] // 2
    rank_local = w_query_down.shape[1]
    rank_full = w_query_up.shape[0]
    width_local = model_width // groups
    keyvalue_local = 2 * head_dim // groups
    block_rows = min(512, seq_len)
    assert seq_count == 1
    cosines, sines = lane_angles(seq_len, head_dim)
    key_live = jnp.arange(seq_len)[None, :] < lengths[:, None]
    valid_rows = key_live.reshape(tokens, 1)
    inputs_f = inputs.astype(jnp.float32)
    inverse_one = lax.rsqrt(jnp.mean(inputs_f * inputs_f, axis=-1, keepdims=True) + epsilon)
    normed = (gain_one * inputs_f * inverse_one).astype(jnp.bfloat16)
    latent = jnp.dot(normed, w_query_down, preferred_element_type=jnp.float32).astype(jnp.bfloat16)
    latent_f = latent.astype(jnp.float32)
    gain_slice = lax.dynamic_slice_in_dim(gain_query, member * rank_local, rank_local)
    latent_whole = gather_over_tensor(latent).astype(jnp.float32)
    inverse_query = lax.rsqrt(
        jnp.mean(latent_whole * latent_whole, axis=-1, keepdims=True) + epsilon
    )
    latent_normed = (gain_query * latent_whole * inverse_query).astype(jnp.bfloat16)
    key_rows, value_rows = project_keyvalue(normed, w_keyvalue, cosines, sines)
    query_parts, context_parts = [], []
    for part in range(seq_len // block_rows):
        query_part, context_part = attend(
            part, block_rows, lengths, latent_normed, w_query_up, key_rows, value_rows,
            cosines, sines,
        )
        query_parts.append(query_part)
        context_parts.append(context_part)
    context = jnp.concatenate(context_parts, axis=0)
    part_rows = seq_count * block_rows
    parts = range(len(context_parts))

    def rows_of(values, part):
        return values[part * part_rows : (part + 1) * part_rows]

    attention_parts = [
        sum_over_tensor(
            jnp.dot(
                context_parts[part], w_output, preferred_element_type=jnp.float32
            ).astype(jnp.bfloat16),
        )
        for part in parts
    ]
    residuals, inverses, normed_twos, hiddens = [], [], [], []
    gates, ups, differs, grad_outs = [], [], [], []
    for part in parts:
        attention_part = attention_parts[part]
        if part > 0:
            attention_part, hiddens[-1] = lax.optimization_barrier((attention_part, hiddens[-1]))
        residual = rows_of(inputs_f, part) + attention_part.astype(jnp.float32)
        inverse_two = lax.rsqrt(jnp.mean(residual * residual, axis=-1, keepdims=True) + epsilon)
        normed_two = (gain_two * residual * inverse_two).astype(jnp.bfloat16)
        gate_values = jnp.dot(normed_two, w_gate, preferred_element_type=jnp.float32)
        up_values = jnp.dot(normed_two, w_up, preferred_element_type=jnp.float32)
        hidden = (gate_values * jax.nn.sigmoid(gate_values) * up_values).astype(jnp.bfloat16)
        feed = jnp.dot(hidden, w_down, preferred_element_type=jnp.float32).astype(jnp.bfloat16)
        feed_share = scatter_over_tensor(feed).astype(jnp.float32)
        residual_share = lax.dynamic_slice_in_dim(residual, member * width_local, width_local, 1)
        output = (residual_share + feed_share).astype(jnp.bfloat16)
        differ = jnp.where(
            rows_of(valid_rows, part),
            output.astype(jnp.float32) - rows_of(teacher, part).astype(jnp.float32),
            0.0,
        )
        residuals.append(residual)
        inverses.append(inverse_two)
        normed_twos.append(normed_two)
        hiddens.append(hidden)
        gates.append(gate_values)
        ups.append(up_values)
        differs.append((output, differ))
        grad_outs.append(gather_over_tensor(differ.astype(jnp.bfloat16)))
    output = jnp.concatenate([pair[0] for pair in differs], axis=0)
    differ = jnp.concatenate([pair[1] for pair in differs], axis=0)
    normed_two = jnp.concatenate(normed_twos, axis=0)
    error_part = jnp.sum(differ * differ, keepdims=True).reshape(1)
    gate_grads, up_grads, part_sums = [], [], []
    for part in parts:
        gate_values, up_values = gates[part], ups[part]
        if part > 0:
            grad_outs[part], gate_grads[-1], up_grads[-1] = lax.optimization_barrier(
                (grad_outs[part], gate_grads[-1], up_grads[-1])
            )
        sigmoid_gate = jax.nn.sigmoid(gate_values)
        grad_hidden = jnp.einsum(
            "td,fd->tf", grad_outs[part], w_down, preferred_element_type=jnp.float32
        )
        gate_grad = (
            grad_hidden * up_values * sigmoid_gate * (1.0 + gate_values * (1.0 - sigmoid_gate))
        ).astype(jnp.bfloat16)
        up_grad = (grad_hidden * gate_values * sigmoid_gate).astype(jnp.bfloat16)
        gate_grads.append(gate_grad)
        up_grads.append(up_grad)
        part_sum = (
            jnp.einsum("tf,kf->tk", gate_grad, w_gate, preferred_element_type=jnp.float32)
            + jnp.einsum("tf,kf->tk", up_grad, w_up, preferred_element_type=jnp.float32)
        ).astype(jnp.bfloat16)
        part_sums.append(sum_over_tensor(part_sum))
    gate_grad = jnp.concatenate(gate_grads, axis=0)
    up_grad = jnp.concatenate(up_grads, axis=0)
    grad_w_gate = jnp.einsum("tk,tf->kf", normed_two, gate_grad, preferred_element_type=jnp.float32)
    grad_w_up = jnp.einsum("tk,tf->fk", normed_two, up_grad, preferred_element_type=jnp.float32)
    grad_w_down = sum(
        jnp.einsum("tf,td->fd", hiddens[part], grad_outs[part], preferred_element_type=jnp.float32)
        for part in parts
    )
    grad_gain_two = 0.0
    residual_lows, residual_shares, grad_contexts = [], [], []
    for part in parts:
        residual, inverse_two = residuals[part], inverses[part]
        part_sum = part_sums[part]
        if part > 0:
            part_sum, grad_contexts[-1] = lax.optimization_barrier((part_sum, grad_contexts[-1]))
        grad_normed_two = part_sum.astype(jnp.float32)
        scaled_two = gain_two * grad_normed_two
        grad_residual = (
            grad_outs[part].astype(jnp.float32)
            + inverse_two * scaled_two
            - residual * inverse_two**3 * jnp.mean(scaled_two * residual, axis=-1, keepdims=True)
        )
        grad_gain_two = grad_gain_two + jnp.sum(grad_normed_two * residual * inverse_two, axis=0)
        grad_residual_low = grad_residual.astype(jnp.bfloat16)
        residual_lows.append(grad_residual_low)
        residual_shares.append(
            lax.dynamic_slice_in_dim(grad_residual, member * width_local, width_local, 1)
        )
        grad_contexts.append(
            jnp.einsum(
                "td,cd->tc", grad_residual_low, w_output, preferred_element_type=jnp.float32
            ).astype(jnp.bfloat16)
        )
    grad_gain_two = lax.dynamic_slice_in_dim(grad_gain_two, member * width_local, width_local)
    grad_residual_low = jnp.concatenate(residual_lows, axis=0)
    residual_grad_share = jnp.concatenate(residual_shares, axis=0)
    grad_w_output = jnp.einsum(
        "tc,td->cd", context, grad_residual_low, preferred_element_type=jnp.float32
    )
    query_grads, earlier = [], []
    for part in parts:
        query_grad, keyvalue_part = attend_back(
            part, block_rows, part == parts[-1], lengths, query_parts[part], grad_contexts[part],
            key_rows, value_rows, cosines, sines, earlier,
        )
        query_grads.append(query_grad)
        earlier = [keyvalue_part]
    grad_query_pre = jnp.concatenate(query_grads, axis=0)
    grad_w_query_up = jnp.einsum(
        "tr,tc->rc", latent_normed, grad_query_pre, preferred_element_type=jnp.float32
    )
    latent_part = jnp.einsum(
        "tc,rc->tr", grad_query_pre, w_query_up, preferred_element_type=jnp.float32
    )
    grad_keyvalue = scatter_over_tensor(keyvalue_part)
    (latent_dots,) = sum_small([jnp.sum(gain_query * latent_part * latent_whole, axis=-1)])
    latent_share = scatter_over_tensor(latent_part.astype(jnp.bfloat16)).astype(jnp.float32)
    w_keyvalue_share = lax.dynamic_slice_in_dim(
        w_keyvalue, member * keyvalue_local, keyvalue_local, 1
    )
    grad_w_keyvalue = jnp.einsum(
        "tk,tc->kc", normed, grad_keyvalue, preferred_element_type=jnp.float32
    )
    scaled_latent = gain_slice * latent_share
    grad_gain_query = jnp.sum(latent_share * latent_f * inverse_query, axis=0)
    grad_latent = (
        inverse_query * scaled_latent
        - latent_f * inverse_query**3 * (latent_dots / rank_full)[:, None]
    ).astype(jnp.bfloat16)
    grad_w_query_down = jnp.einsum(
        "tk,tr->kr", normed, grad_latent, preferred_element_type=jnp.float32
    )
    normed_part = jnp.einsum(
        "tr,kr->tk", grad_latent, w_query_down, preferred_element_type=jnp.float32
    ) + jnp.einsum("tc,kc->tk", grad_keyvalue, w_keyvalue_share, preferred_element_type=jnp.float32)
    input_dots, gain_one_sums, error_part = sum_small(
        [
            jnp.sum(gain_one * normed_part * inputs_f, axis=-1),
            jnp.sum(normed_part * inputs_f * inverse_one, axis=0),
            error_part,
        ]
    )
    grad_gain_one = lax.dynamic_slice_in_dim(gain_one_sums, member * width_local, width_local)
    dp_size = lax.axis_size("dp")
    own_slot = (jnp.arange(dp_size) == lax.axis_index("dp"))[:, None]
    scalar_parts = jnp.stack(
        exact_parts(error_part[0], 3) + exact_parts(jnp.sum(lengths).astype(jnp.float32), 2)
    )
    small_row = jnp.concatenate(
        [
            grad_gain_one,
            grad_gain_query,
            grad_gain_two,
            jnp.where(own_slot, scalar_parts[None, :], 0.0).reshape(5 * dp_size),
        ]
    ).astype(jnp.bfloat16)
    small = jnp.pad(
        small_row[None, :], ((0, 2 * chunk_rows - 1), (0, model_width - small_row.shape[0]))
    )
    normed_pieces = scatter_step(
        jnp.split(normed_part.astype(jnp.bfloat16), groups, axis=1), tensor_masks()[0]
    )
    summands = [
        grad_w_down.astype(jnp.bfloat16),
        grad_w_up.astype(jnp.bfloat16),
        grad_w_output.astype(jnp.bfloat16),
        fold_rows(grad_w_query_up.astype(jnp.bfloat16), model_width),
        fold_rows(grad_w_query_down.astype(jnp.bfloat16), model_width),
        fold_rows(grad_w_keyvalue.astype(jnp.bfloat16), model_width),
        small,
    ]
    summands = lax.optimization_barrier((summands, normed_pieces))[0]
    for mask in tensor_masks()[1:]:
        normed_pieces = scatter_step(normed_pieces, mask)
    grad_normed = normed_pieces[0].astype(jnp.float32)
    dp_totals = sum_over_dp(summands)
    (
        down_total, up_total, output_total, query_up_total, query_down_total, keyvalue_total, small_total,
    ) = dp_totals
    grad_gain_one, grad_gain_query, grad_gain_two, scalar_sums = jnp.split(
        small_total[0, : small_row.shape[0]].astype(jnp.float32),
        [width_local, width_local + rank_local, 2 * width_local + rank_local],
    )
    scalar_sums = scalar_sums.reshape(dp_size, 5)
    valid_count = jnp.sum(scalar_sums[:, 3:])
    layer_loss = jnp.sum(scalar_sums[:, :3]) / (valid_count * model_width)
    grad_scale = float(tokens * dp_size) / valid_count
    grad_gain_one, grad_gain_query, grad_gain_two = (
        values * grad_scale for values in (grad_gain_one, grad_gain_query, grad_gain_two)
    )
    inputs_share = lax.dynamic_slice_in_dim(inputs_f, member * width_local, width_local, 1)
    gain_share = lax.dynamic_slice_in_dim(gain_one, member * width_local, width_local)
    scaled_one = gain_share * grad_normed
    input_grad = (
        grad_scale
        * (
            residual_grad_share
            + inverse_one * scaled_one
            - inputs_share * inverse_one**3 * (input_dots / model_width)[:, None]
        )
    ).astype(jnp.bfloat16)
    weight_grads = {}
    weight_grads["gate"] = lax.psum(grad_w_gate.astype(jnp.bfloat16), "dp")
    weight_grads["down"] = down_total
    weight_grads["output"] = output_total
    weight_grads["query_up"] = unfold_rows(query_up_total, w_query_up.shape[1])
    weight_grads["query_down"] = unfold_rows(query_down_total, rank_local)
    weight_grads["keyvalue"] = unfold_rows(keyvalue_total, keyvalue_local)
    weight_grads = {
        name: values.astype(jnp.float32) * grad_scale for name, values in weight_grads.items()
    }
    grad_w_down, grad_w_gate, grad_w_output = (
        weight_grads[name] for name in ("down", "gate", "output")
    )
    if up_total.shape[0] % 128 == 0:
        grad_w_up = transpose_scaled(up_total, grad_scale)
    else:
        grad_w_up = up_total.T.astype(jnp.float32) * grad_scale
    grad_w_query_up, grad_w_query_down, grad_w_keyvalue = (
        weight_grads[name] for name in ("query_up", "query_down", "keyvalue")
    )
    return (
        output,
        layer_loss,
        input_grad,
        grad_gain_one,
        grad_w_query_down,
        grad_gain_query,
        grad_w_query_up,
        grad_w_keyvalue,
        grad_w_output,
        grad_gain_two,
        grad_w_gate,
        grad_w_up,
        grad_w_down,
    )


def solution(mesh):
    placed = (
        P("dp", None),
        P("dp", "tensor"),
        P("dp"),
        P(),
        P(None, "tensor"),
        P(),
        P(None, "tensor"),
        P(),
        P("tensor", None),
        P(),
        P(None, "tensor"),
        P(None, "tensor"),
        P("tensor", None),
    )
    return jax.shard_map(
        layer,
        mesh=mesh,
        in_specs=placed,
        out_specs=(
            P("dp", "tensor"),
            P(),
            P("dp", "tensor"),
            P("tensor"),
            P(None, "tensor"),
            P("tensor"),
            P(None, "tensor"),
            P(None, "tensor"),
            P("tensor", None),
            P("tensor"),
            P(None, "tensor"),
            P(None, "tensor"),
            P("tensor", None),
        ),
        check_vma=False,
    )
```
